32 devices in a mesh: pair: 8 (over y, x, core), tile: 4 (over z).
Axes of the slice: x: 2, y: 2, z: 4, core: 2. Of those that a mesh axis runs over, the one named last changes fastest.
Arguments:
- fixed: float32 [4096, 512], P('pair', 'tile'), parts along dimension 0, may hold values from -6 to 6
- moving: float32 [4096, 512], P('pair', 'tile'), parts along dimension 0, may hold values from -6 to 6
- offsets: int32 [2, 4096, 512], P(None, ('pair', 'tile')), parts along dimension 1, may hold values from -3 to 3
- fractions: float32 [2, 4096, 512], P(None, ('pair', 'tile')), parts along dimension 1, may hold values from 0 to 1
Outputs:
- warped: float32 [4096, 512], P(('pair', 'tile')), parts along dimension 0
The draws below stay inside these ranges and needn't reach their ends.
There are 8 independent parts, one for each index of `pair`. The reference program is written for one: setup_inputs(seed, part) draws one part's arguments, and reference() takes and returns one part's arrays. A program takes and returns all parts, laid end to end along the dimension named above; each array names one. Nothing has to cross between parts.
All inputs are finite; a program needn't handle non-finite values.
Results may differ from the reference program's by a relative error of at most 0.00002.
Values sent between devices are 32-bit elements; how exact they have to be, the bound alone decides.
No kernel may reach another device: no remote copies, remote signals or barrier semaphores. Data moves between devices by JAX's collectives and lax.ppermute only.
A program may use at most 64 MiB of HBM per device.

```python
import jax
import jax.numpy as jnp

RADIUS = 4
REACH = 3
HEIGHT = 512
WIDTH = 512


def touch_ends(values, own_key, least, largest):
    place = [jax.random.randint(jax.random.fold_in(own_key, axis), (), 0, length) for axis, length in enumerate(values.shape)]
    longest = values.shape.index(max(values.shape))
    beside = place[:longest] + [(place[longest] + 1) % values.shape[longest]] + place[longest + 1:]
    return values.at[tuple(place)].set(least).at[tuple(beside)].set(largest)


def shard_levels(rng, dims, pieces, least, high):
    gain = 1.0
    for position, shards_of in pieces:
        draws = jax.random.uniform(jax.random.fold_in(jax.random.fold_in(rng, 6), position), (shards_of,), jnp.float32, least / len(pieces), high / len(pieces))
        gain = gain * jnp.repeat(jnp.exp(draws), dims[position] // shards_of).reshape((-1,) + (1,) * (len(dims) - 1 - position))
    return gain


def normal_values(own_key, dims, scale, most, shards=(), kind=jnp.bfloat16):
    values = jax.random.normal(own_key, dims, jnp.float32) * scale
    if len(shards) > 0:
        values = shard_levels(own_key, dims, shards, -0.22, 0.18) * values
    return jnp.clip(values, min=-most, max=most).astype(kind)


def setup_inputs(seed: int = 0, part: int = 0) -> dict:
    keys = jax.random.split(jax.random.key(seed), 5)
    own_keys = jax.random.split(jax.random.fold_in(keys[4], part), 5)
    return {
        "fixed": normal_values(own_keys[0], (HEIGHT, WIDTH), 1.0, 6.0, ((1, 4),), jnp.float32),
        "moving": normal_values(own_keys[1], (HEIGHT, WIDTH), 1.0, 6.0, ((1, 4),), jnp.float32),
        "offsets": touch_ends(jax.random.randint(own_keys[2], (2, HEIGHT, WIDTH), -REACH, REACH + 1), jax.random.fold_in(own_keys[2], 1), -REACH, REACH).astype(jnp.int32),
        "fractions": jnp.clip(1.0 * jax.random.uniform(own_keys[3], (2, HEIGHT, WIDTH), jnp.float32) ** shard_levels(own_keys[3], (2, HEIGHT, WIDTH), ((1, 4),), -0.2, 0.2), 0.0, 1.0),
    }


def window_sum(extended):
    row_total = extended.shape[0] - 2 * RADIUS
    column_total = extended.shape[1] - 2 * RADIUS
    rows_summed = extended[0:row_total, :]
    for shift in range(1, 2 * RADIUS + 1):
        rows_summed = rows_summed + extended[shift:shift + row_total, :]
    result = rows_summed[:, 0:column_total]
    for shift in range(1, 2 * RADIUS + 1):
        result = result + rows_summed[:, shift:shift + column_total]
    return result

def similarity(fixed_ext, moving_ext):
    window_count = float((2 * RADIUS + 1) ** 2)
    fixed_sum = window_sum(fixed_ext)
    moving_sum = window_sum(moving_ext)
    fixed_square = window_sum(fixed_ext * fixed_ext)
    moving_square = window_sum(moving_ext * moving_ext)
    cross_sum = window_sum(fixed_ext * moving_ext)
    fixed_var = fixed_square - fixed_sum * fixed_sum / window_count
    moving_var = moving_square - moving_sum * moving_sum / window_count
    covariance = cross_sum - fixed_sum * moving_sum / window_count
    correlation = covariance / jnp.sqrt(fixed_var * moving_var + 0.001)
    return 0.5 * (1.0 + correlation)

def reference(fixed, moving, offsets, fractions):
    confidence = similarity(jnp.pad(fixed, RADIUS), jnp.pad(moving, RADIUS))
    margin = REACH + 1
    padded = jnp.pad(moving, margin)
    row_index = jnp.arange(HEIGHT, dtype=jnp.int32)[:, None] + offsets[0] + margin
    column_index = jnp.arange(WIDTH, dtype=jnp.int32)[None, :] + offsets[1] + margin
    top_left = padded[row_index, column_index]
    top_right = padded[row_index, column_index + 1]
    bottom_left = padded[row_index + 1, column_index]
    bottom_right = padded[row_index + 1, column_index + 1]
    row_weight = confidence * fractions[0]
    column_weight = confidence * fractions[1]
    upper = (1.0 - column_weight) * top_left + column_weight * top_right
    lower = (1.0 - column_weight) * bottom_left + column_weight * bottom_right
    return (1.0 - row_weight) * upper + row_weight * lower
```

```python
import functools

import jax
import jax.numpy as jnp
from jax import lax
from jax.experimental import pallas as pl
from jax.experimental.pallas import tpu as pltpu
from jax.sharding import PartitionSpec as P

RADIUS = 4
REACH = 3
HALO = max(RADIUS, REACH + 1)
LANES = 128
SUB = 8
F32 = jnp.float32


def hops(n):
    middle = n // 2
    return [middle] + [k for k in range(1, n) if k != middle]


def pack_band(strip, out, band, n, rows):
    top = strip[pl.ds(pl.multiple_of(jnp.maximum(band * rows - SUB, 0), SUB), SUB), :]
    out[0:HALO, :] = jnp.where(band > 0, top, 0.0)[SUB - HALO :, :]
    start = pl.multiple_of(band * rows, SUB)
    out[HALO : HALO + rows, :] = strip[pl.ds(start, rows), :]
    low = strip[pl.ds(pl.multiple_of(jnp.minimum(start + rows, n * rows - SUB), SUB), SUB), :]
    out[HALO + rows :, :] = jnp.where(band < n - 1, low, 0.0)[:HALO, :]


def pack_kernel(n, rows, moving, fixed, *refs):
    outs, (mbuf, fbuf, sem) = refs[: 2 * n], refs[2 * n :]
    me = lax.axis_index("tile")
    copies = [
        pltpu.make_async_copy(moving, mbuf, sem.at[0]),
        pltpu.make_async_copy(fixed, fbuf, sem.at[1]),
    ]
    for copy in copies:
        copy.start()
    for image, buf in enumerate((mbuf, fbuf)):
        copies[image].wait()
        for place, k in enumerate(hops(n) + [0]):
            pack_band(buf, outs[image * n + place], lax.rem(me + k, n), n, rows)


def row_sums(load, g):
    total = load(g * SUB)
    for shift in range(1, 2 * RADIUS + 1):
        total = total + load(g * SUB + shift)
    return total


def column_sums(x):
    size = x.shape[1]
    pairs = x + pltpu.roll(x, size - 1, 1)
    fours = pairs + pltpu.roll(pairs, size - 2, 1)
    return fours + pltpu.roll(fours, 4, 1) + pltpu.roll(x, size - 4, 1)


def pick(values, low, high, top):
    even = jnp.where(high, jnp.where(top, values[6], values[4]), jnp.where(top, values[2], values[0]))
    odd = jnp.where(high, jnp.where(top, values[7], values[5]), jnp.where(top, values[3], values[1]))
    after = jnp.where(high, values[6], jnp.where(top, values[4], values[2]))
    return jnp.where(low, odd, even), jnp.where(low, after, odd)


def moving_kernel(n, rows, width, *refs):
    blocks, offsets, fractions = refs[:n], refs[n], refs[n + 1]
    base, linear, square, msum, mvar = refs[n + 2 : n + 7]
    wide, side, sq, rs, rsq, obuf, fbuf, sem = refs[n + 7 :]
    me = lax.axis_index("tile")
    copies = [
        pltpu.make_async_copy(offsets, obuf, sem.at[0]),
        pltpu.make_async_copy(fractions, fbuf, sem.at[1]),
    ]
    for copy in copies:
        copy.start()
    deep = rows + 2 * HALO
    count = float((2 * RADIUS + 1) ** 2)
    rs[:, width:] = jnp.zeros((rows, LANES), F32)
    rsq[:, width:] = jnp.zeros((rows, LANES), F32)
    wide[n] = jnp.zeros((deep, LANES), F32)
    for place, k in enumerate(hops(n) + [0]):
        block = blocks[place]
        source = lax.rem(me - k + n, n)
        wide[source] = block[...]
        sq[...] = block[...] * block[...]
        at = pl.ds(pl.multiple_of(source * LANES, LANES), LANES)
        for g in range(rows // SUB):
            out_rows = slice(g * SUB, (g + 1) * SUB)
            rs[out_rows, at] = row_sums(lambda y: block[y : y + SUB, :], g)
            rsq[out_rows, at] = row_sums(lambda y: sq[y : y + SUB, :], g)
    for g in range(rows // SUB):
        out_rows = slice(g * SUB, (g + 1) * SUB)
        total = column_sums(rs[out_rows, :])[:, :width]
        squares = column_sums(rsq[out_rows, :])[:, :width]
        msum[out_rows, :] = total
        mvar[out_rows, :] = squares - total * total * (1.0 / count)
    lane_deep = lax.broadcasted_iota(jnp.int32, (deep, LANES), 1)
    for s in range(n):
        side[s] = jnp.where(
            lane_deep < LANES // 2, wide[s + 1], wide[s - 1 if s else n]
        )
    for copy in copies:
        copy.wait()
    lane = lax.broadcasted_iota(jnp.int32, (SUB, LANES), 1)

    def unit(g, s):
        y0 = g * SUB
        at = pl.ds(s * LANES, LANES)
        down = obuf[0, y0 : y0 + SUB, at] + REACH
        left = lane + obuf[1, y0 : y0 + SUB, at]
        right = left + 1
        left_in = (left & (LANES - 1)) == left
        right_in = (right & (LANES - 1)) == right
        left = left & (LANES - 1)
        right = right & (LANES - 1)
        lefts, rights = [], []
        take = functools.partial(jnp.take_along_axis, axis=1, mode="promise_in_bounds")
        for r in range(2 * REACH + 2):
            e = y0 + r + HALO - REACH
            own = wide[s, e : e + SUB, :]
            other = side[s, e : e + SUB, :]
            lefts.append(jnp.where(left_in, take(own, left), take(other, left)))
            rights.append(jnp.where(right_in, take(own, right), take(other, right)))
        low = (down & 1) == 1
        high = down >= 4
        top = (down & 2) == 2
        top_left, bottom_left = pick(lefts, low, high, top)
        top_right, bottom_right = pick(rights, low, high, top)
        rf = fbuf[0, y0 : y0 + SUB, at]
        cf = fbuf[1, y0 : y0 + SUB, at]
        across = top_right - top_left
        base[y0 : y0 + SUB, at] = top_left
        linear[y0 : y0 + SUB, at] = cf * across + rf * (bottom_left - top_left)
        square[y0 : y0 + SUB, at] = (rf * cf) * ((bottom_right - bottom_left) - across)

    for g in range(rows // SUB):
        for s in range(n):
            unit(g, s)


def final_kernel(n, rows, width, *refs):
    fixed, moving = refs[:n], refs[n : 2 * n]
    base, linear, square, msum, mvar, out = refs[2 * n : 2 * n + 6]
    sums, ff, fm, obuf, sem = refs[2 * n + 6 :]
    me = lax.axis_index("tile")
    inv = 1.0 / float((2 * RADIUS + 1) ** 2)
    for which in range(3):
        sums[which, :, width:] = jnp.zeros((rows, LANES), F32)
    for place, k in enumerate(hops(n) + [0]):
        f, m = fixed[place], moving[place]
        source = lax.rem(me - k + n, n)
        ff[...] = f[...] * f[...]
        fm[...] = f[...] * m[...]
        at = pl.ds(pl.multiple_of(source * LANES, LANES), LANES)
        for g in range(rows // SUB):
            out_rows = slice(g * SUB, (g + 1) * SUB)
            for which, ref in enumerate((f, ff, fm)):
                sums[which, out_rows, at] = row_sums(lambda y: ref[y : y + SUB, :], g)
    chunks = 4
    per = rows // chunks
    copies = []
    for chunk in range(chunks):
        for g in range(chunk * per // SUB, (chunk + 1) * per // SUB):
            out_rows = slice(g * SUB, (g + 1) * SUB)
            fsum = column_sums(sums[0, out_rows, :])[:, :width]
            fsq = column_sums(sums[1, out_rows, :])[:, :width]
            cross = column_sums(sums[2, out_rows, :])[:, :width]
            ms = msum[out_rows, :]
            fvar = fsq - fsum * fsum * inv
            cov = cross - fsum * ms * inv
            conf = 0.5 + 0.5 * (cov * lax.rsqrt(fvar * mvar[out_rows, :] + 0.001))
            obuf[out_rows, :] = base[out_rows, :] + conf * (
                linear[out_rows, :] + conf * square[out_rows, :]
            )
        copy = pltpu.make_async_copy(
            obuf.at[pl.ds(chunk * per, per), :], out.at[pl.ds(chunk * per, per), :], sem.at[chunk]
        )
        copy.start()
        copies.append(copy)
    for copy in copies:
        copy.wait()


VMEM = pl.BlockSpec(memory_space=pltpu.VMEM)
ANY = pl.BlockSpec(memory_space=pl.ANY)


def on_device(n, fixed, moving, offsets, fractions):
    rows, width = offsets.shape[1:]
    strip = moving.shape
    deep = rows + 2 * HALO
    band = jax.ShapeDtypeStruct((deep, strip[1]), F32)
    plane = jax.ShapeDtypeStruct((rows, width), F32)
    packed = pl.pallas_call(
        functools.partial(pack_kernel, n, rows),
        out_shape=[band] * (2 * n),
        in_specs=[ANY] * 2,
        out_specs=[VMEM] * (2 * n),
        scratch_shapes=[pltpu.VMEM(strip, F32)] * 2 + [pltpu.SemaphoreType.DMA((2,))],
        name="pack",
    )(moving, fixed)
    order = hops(n)

    def send(blocks):
        got = [
            lax.ppermute(block, "tile", [(i, (i + k) % n) for i in range(n)])
            for block, k in zip(blocks, order)
        ]
        return got + [blocks[-1]]

    moved = send(packed[:n])
    fixes = send(packed[n:])
    parts = pl.pallas_call(
        functools.partial(moving_kernel, n, rows, width),
        out_shape=[plane] * 5,
        in_specs=[VMEM] * n + [ANY] * 2,
        out_specs=[VMEM] * 5,
        scratch_shapes=[
            pltpu.VMEM((n + 1, deep, LANES), F32),
            pltpu.VMEM((n, deep, LANES), F32),
            pltpu.VMEM((deep, LANES), F32),
            pltpu.VMEM((rows, width + LANES), F32),
            pltpu.VMEM((rows, width + LANES), F32),
            pltpu.VMEM(offsets.shape, jnp.int32),
            pltpu.VMEM(fractions.shape, F32),
            pltpu.SemaphoreType.DMA((2,)),
        ],
        cost_estimate=pl.CostEstimate(
            flops=200 * rows * width, bytes_accessed=16 * rows * width, transcendentals=0
        ),
        name="moving_part",
    )(*moved, offsets, fractions)
    return pl.pallas_call(
        functools.partial(final_kernel, n, rows, width),
        out_shape=plane,
        in_specs=[VMEM] * (2 * n + 5),
        out_specs=ANY,
        scratch_shapes=[
            pltpu.VMEM((3, rows, width + LANES), F32),
            pltpu.VMEM((deep, LANES), F32),
            pltpu.VMEM((deep, LANES), F32),
            pltpu.VMEM((rows, width), F32),
            pltpu.SemaphoreType.DMA((4,)),
        ],
        name="final_part",
    )(*fixes, *moved, *parts)


def solution(mesh):
    placed = (
        P("pair", "tile"),
        P("pair", "tile"),
        P(None, ("pair", "tile"), None),
        P(None, ("pair", "tile"), None),
    )
    return jax.shard_map(
        functools.partial(on_device, mesh.shape["tile"]),
        mesh=mesh,
        in_specs=placed,
        out_specs=P(("pair", "tile"), None),
        check_vma=False,
    )
```

```python
import functools

import jax
import jax.numpy as jnp
from jax import lax
from jax.experimental import pallas as pl
from jax.experimental.pallas import tpu as pltpu
from jax.sharding import PartitionSpec as P

RADIUS = 4
REACH = 3
HALO = max(RADIUS, REACH + 1)
LANES = 128
SUB = 8
F32 = jnp.float32
BF16 = jnp.bfloat16
ROOM = 28 * 2**20


def hops(n):
    middle = n // 2
    return [middle] + [k for k in range(1, n) if k != middle]


def pack_band(strip, out, band, n, rows):
    top = strip[pl.ds(pl.multiple_of(jnp.maximum(band * rows - SUB, 0), SUB), SUB), :]
    out[0:HALO, :] = jnp.where(band > 0, top, 0.0)[SUB - HALO :, :]
    start = pl.multiple_of(band * rows, SUB)
    out[HALO : HALO + rows, :] = strip[pl.ds(start, rows), :]
    low = strip[pl.ds(pl.multiple_of(jnp.minimum(start + rows, n * rows - SUB), SUB), SUB), :]
    out[HALO + rows :, :] = jnp.where(band < n - 1, low, 0.0)[:HALO, :]


def pack_kernel(n, rows, moving, fixed, *refs):
    outs, (mbuf, fbuf, sem) = refs[: 2 * n], refs[2 * n :]
    me = lax.axis_index("tile")
    copies = [
        pltpu.make_async_copy(moving, mbuf, sem.at[0]),
        pltpu.make_async_copy(fixed, fbuf, sem.at[1]),
    ]
    for copy in copies:
        copy.start()
    for image, buf in enumerate((mbuf, fbuf)):
        copies[image].wait()
        for place, k in enumerate(hops(n) + [0]):
            pack_band(buf, outs[image * n + place], lax.rem(me + k, n), n, rows)


def row_sums(ref, out, rows):
    for g in range((rows + SUB) // SUB):
        y = g * SUB
        last = min(SUB, rows + 6 - y)
        out[y : y + last, :] = (
            ref[y : y + last, :] + ref[y + 1 : y + 1 + last, :] + ref[y + 2 : y + 2 + last, :]
        )

    def total(y, size):
        return out[y : y + size, :] + out[y + 3 : y + 3 + size, :] + out[y + 6 : y + 6 + size, :]

    return total


def split(x):
    high = x.astype(BF16)
    rest = x - high.astype(F32)
    middle = rest.astype(BF16)
    low = (rest - middle.astype(F32)).astype(BF16)
    return high, middle, low


def put(terms, source, y, x):
    at = pl.ds(pl.multiple_of((source + 1) * LANES, LANES), LANES)
    for t, part in enumerate(split(x)):
        terms[t, y : y + x.shape[0], at] = part


def clear_ends(terms):
    zeros = jnp.zeros((terms.shape[1], LANES), BF16)
    for t in range(3):
        terms[t, :, :LANES] = zeros
        terms[t, :, terms.shape[2] - LANES :] = zeros


def lane_sums(arrays, width, size, weights):
    wide = size + 2 * LANES
    left = [
        jnp.concatenate([terms[t, :, start : start + wide] for t in range(3)], axis=1)
        for terms in arrays
        for start in range(0, width, size)
    ]
    out = jnp.dot(jnp.concatenate(left, axis=0), weights, preferred_element_type=F32)
    rows = arrays[0].shape[1]
    parts = [out[i * rows : (i + 1) * rows] for i in range(len(left))]
    count = width // size
    return [parts[i * count : (i + 1) * count] for i in range(len(arrays))]


def band_matrix(first, last, size):
    shape = (size + 2 * LANES, size)
    source = lax.broadcasted_iota(jnp.int32, shape, 0)
    target = lax.broadcasted_iota(jnp.int32, shape, 1)
    distance = source - target - LANES
    band = jnp.where((distance >= first) & (distance <= last), 1.0, 0.0).astype(BF16)
    return jnp.concatenate([band] * 3, axis=0)


def narrow(values, bit):
    return [jnp.where(bit, values[i + 4], values[i]) for i in range(4)] + [values[4]]


def moving_kernel(n, rows, width, *refs):
    blocks, offsets, fractions = refs[:n], refs[n], refs[n + 1]
    base, linear, square, msum, mvar = refs[n + 2 : n + 7]
    image, sums, squares, shifted, sq, three, obuf, fbuf, sem = refs[n + 7 :]
    me = lax.axis_index("tile")
    copies = [
        pltpu.make_async_copy(offsets, obuf, sem.at[0]),
        pltpu.make_async_copy(fractions, fbuf, sem.at[1]),
    ]
    for copy in copies:
        copy.start()
    deep = rows + 2 * HALO
    inv = 1.0 / float((2 * RADIUS + 1) ** 2)
    for terms in (sums, squares):
        clear_ends(terms)
    for place, k in enumerate(hops(n) + [0]):
        block = blocks[place]
        source = lax.rem(me - k + n, n)
        for y in range(0, deep, 2 * SUB):
            size = min(2 * SUB, deep - y)
            x = block[y : y + size, :]
            sq[place, y : y + size, :] = x * x
            at = pl.ds(pl.multiple_of(source * LANES, LANES), LANES)
            image[y : y + size, at] = x
        for which, (ref, terms) in enumerate(((block, sums), (sq.at[place], squares))):
            total = row_sums(ref, three.at[which, place], rows)
            for y in range(0, rows, 2 * SUB):
                put(terms, source, y, total(y, 2 * SUB))
    size = LANES * (2 if n % 2 == 0 else 1)
    window = band_matrix(-RADIUS, RADIUS, size)
    totals, seconds = lane_sums((sums, squares), width, size, window)
    for place, (total, second) in enumerate(zip(totals, seconds)):
        at = pl.ds(place * size, size)
        msum[:, at] = total
        mvar[:, at] = second - total * total * inv
    image[:, width:] = jnp.zeros((deep, LANES), F32)
    for y in range(0, deep, SUB):
        x = image[y : y + SUB, :]
        for c in range(-REACH, REACH + 2):
            turned = pltpu.roll(x, (-c) % x.shape[1], 1) if c else x
            for block in range(n):
                shifted[block, c + REACH, y : y + SUB, :] = turned[
                    :, block * LANES : (block + 1) * LANES
                ]
    for copy in copies:
        copy.wait()
    span = 2 * REACH + 2

    def unit(s, y0):
        at = pl.ds(s * LANES, LANES)
        down = obuf[0, y0 : y0 + SUB, at] + REACH
        along = obuf[1, y0 : y0 + SUB, at] + REACH
        down_bits = [down >= 4, (down & 2) == 2, (down & 1) == 1]
        along_bits = [along >= 4, (along & 2) == 2, (along & 1) == 1]

        def load(r):
            e = y0 + r + HALO - REACH
            return [shifted[s, c, e : e + SUB, :] for c in range(span)]

        grid = []
        for r in range(5):
            line = load(r)
            if r < 4:
                line = [jnp.where(down_bits[0], b, a) for a, b in zip(line, load(r + 4))]
            grid.append(narrow(line, along_bits[0]))
        for place, step in ((1, 2), (2, 1)):
            across_bit, down_bit = along_bits[place], down_bits[place]
            lines = [
                [jnp.where(down_bit, b, a) for a, b in zip(grid[r], grid[r + step])]
                for r in range(step + 1)
            ]
            grid = [
                [jnp.where(across_bit, line[i + step], line[i]) for i in range(step + 1)]
                for line in lines
            ]
        (top_left, top_right), (bottom_left, bottom_right) = grid
        rf = fbuf[0, y0 : y0 + SUB, at]
        cf = fbuf[1, y0 : y0 + SUB, at]
        across = top_right - top_left
        base[y0 : y0 + SUB, at] = top_left
        linear[y0 : y0 + SUB, at] = cf * across + rf * (bottom_left - top_left)
        square[y0 : y0 + SUB, at] = (rf * cf) * ((bottom_right - bottom_left) - across)

    for s in range(n):
        for g in range(rows // SUB):
            unit(s, g * SUB)


def final_kernel(n, rows, width, *refs):
    fixed, moving = refs[:n], refs[n : 2 * n]
    base, linear, square, msum, mvar, out = refs[2 * n : 2 * n + 6]
    sums, squares, crosses, ff, fm, three, obuf, sem = refs[2 * n + 6 :]
    me = lax.axis_index("tile")
    inv = 1.0 / float((2 * RADIUS + 1) ** 2)
    for terms in (sums, squares, crosses):
        clear_ends(terms)
    for place, k in enumerate(hops(n) + [0]):
        f, m = fixed[place], moving[place]
        source = lax.rem(me - k + n, n)
        for y in range(0, rows + 2 * HALO, SUB):
            x = f[y : y + SUB, :]
            ff[place, y : y + SUB, :] = x * x
            fm[place, y : y + SUB, :] = x * m[y : y + SUB, :]
        for which, (ref, terms) in enumerate(
            ((f, sums), (ff.at[place], squares), (fm.at[place], crosses))
        ):
            total = row_sums(ref, three.at[which, place], rows)
            for y in range(0, rows, 2 * SUB):
                put(terms, source, y, total(y, 2 * SUB))
    size = LANES * (2 if n % 2 == 0 else 1)
    window = band_matrix(-RADIUS, RADIUS, size)
    copies = []
    windows = lane_sums((sums, squares, crosses), width, size, window)
    for place, (fsum, second, cross) in enumerate(zip(*windows)):
        at = pl.ds(place * size, size)
        fvar = second - fsum * fsum * inv
        cov = cross - fsum * msum[:, at] * inv
        conf = 0.5 + 0.5 * (cov * lax.rsqrt(fvar * mvar[:, at] + 0.001))
        obuf[:, at] = base[:, at] + conf * (linear[:, at] + conf * square[:, at])
        copy = pltpu.make_async_copy(obuf.at[:, at], out.at[:, at], sem.at[place])
        copy.start()
        copies.append(copy)
    for copy in copies:
        copy.wait()


VMEM = pl.BlockSpec(memory_space=pltpu.VMEM)
ANY = pl.BlockSpec(memory_space=pl.ANY)


def held(shape):
    return pltpu.VMEM(shape, F32)


def near(x):
    return pltpu.with_memory_space_constraint(x, pltpu.VMEM)


def on_device(n, fixed, moving, offsets, fractions):
    rows, width = offsets.shape[1:]
    strip = moving.shape
    deep = rows + 2 * HALO
    band = held((deep, strip[1]))
    plane = held((rows, width))
    packed = pl.pallas_call(
        functools.partial(pack_kernel, n, rows),
        out_shape=[band] * (2 * n),
        in_specs=[ANY] * 2,
        out_specs=[VMEM] * (2 * n),
        scratch_shapes=[pltpu.VMEM(strip, F32)] * 2 + [pltpu.SemaphoreType.DMA((2,))],
        compiler_params=pltpu.CompilerParams(vmem_limit_bytes=ROOM),
        name="pack",
    )(moving, fixed)
    order = hops(n)

    def send(blocks):
        got = [
            lax.ppermute(block, "tile", [(i, (i + k) % n) for i in range(n)])
            for block, k in zip(blocks, order)
        ]
        return got + [blocks[-1]]

    moved = send(packed[:n])
    fixes = send(packed[n:])
    parts = pl.pallas_call(
        functools.partial(moving_kernel, n, rows, width),
        out_shape=[plane] * 5,
        in_specs=[VMEM] * n + [ANY] * 2,
        out_specs=[VMEM] * 5,
        scratch_shapes=[
            pltpu.VMEM((deep, width + LANES), F32),
            pltpu.VMEM((3, rows, width + 2 * LANES), BF16),
            pltpu.VMEM((3, rows, width + 2 * LANES), BF16),
            pltpu.VMEM((n, 2 * REACH + 2, deep, LANES), F32),
            pltpu.VMEM((n, deep, LANES), F32),
            pltpu.VMEM((2, n, deep, LANES), F32),
            pltpu.VMEM(offsets.shape, jnp.int32),
            pltpu.VMEM(fractions.shape, F32),
            pltpu.SemaphoreType.DMA((2,)),
        ],
        compiler_params=pltpu.CompilerParams(vmem_limit_bytes=ROOM),
        cost_estimate=pl.CostEstimate(
            flops=200 * rows * width, bytes_accessed=16 * rows * width, transcendentals=0
        ),
        name="moving_part",
    )(*map(near, moved), offsets, fractions)
    return pl.pallas_call(
        functools.partial(final_kernel, n, rows, width),
        out_shape=jax.ShapeDtypeStruct((rows, width), F32),
        in_specs=[VMEM] * (2 * n + 5),
        out_specs=ANY,
        scratch_shapes=[
            pltpu.VMEM((3, rows, width + 2 * LANES), BF16),
            pltpu.VMEM((3, rows, width + 2 * LANES), BF16),
            pltpu.VMEM((3, rows, width + 2 * LANES), BF16),
            pltpu.VMEM((n, deep, LANES), F32),
            pltpu.VMEM((n, deep, LANES), F32),
            pltpu.VMEM((3, n, deep, LANES), F32),
            pltpu.VMEM((rows, width), F32),
            pltpu.SemaphoreType.DMA((n,)),
        ],
        compiler_params=pltpu.CompilerParams(vmem_limit_bytes=ROOM),
        name="final_part",
    )(*map(near, (*fixes, *moved, *parts)))


def solution(mesh):
    placed = (
        P("pair", "tile"),
        P("pair", "tile"),
        P(None, ("pair", "tile"), None),
        P(None, ("pair", "tile"), None),
    )
    return jax.shard_map(
        functools.partial(on_device, mesh.shape["tile"]),
        mesh=mesh,
        in_specs=placed,
        out_specs=P(("pair", "tile"), None),
        check_vma=False,
    )
```

```python
import functools

import jax
import jax.numpy as jnp
from jax import lax
from jax.experimental import pallas as pl
from jax.experimental.pallas import tpu as pltpu
from jax.sharding import PartitionSpec as P

RADIUS = 4
REACH = 3
HALO = max(RADIUS, REACH + 1)
LANES = 128
SUB = 8
F32 = jnp.float32
BF16 = jnp.bfloat16
ROOM = 28 * 2**20


def hops(n):
    middle = n // 2
    return [middle] + [k for k in range(1, n) if k != middle]


def pack_band(strip, base, out, band, n, rows):
    start = pl.multiple_of(band * rows - base, SUB)
    size = strip.shape[0]
    top = strip[pl.ds(pl.multiple_of(jnp.maximum(start - SUB, 0), SUB), SUB), :]
    out[0:HALO, :] = jnp.where(band > 0, top, 0.0)[SUB - HALO :, :]
    out[HALO : HALO + rows, :] = strip[pl.ds(start, rows), :]
    low = strip[pl.ds(pl.multiple_of(jnp.minimum(start + rows, size - SUB), SUB), SUB), :]
    out[HALO + rows :, :] = jnp.where(band < n - 1, low, 0.0)[:HALO, :]


def first_kernel(n, rows, pieces, moving, out, window, sem):
    band = lax.rem(lax.axis_index("tile") + hops(n)[0], n)
    size = window.shape[0]
    base = pl.multiple_of(jnp.clip(band * rows - SUB, 0, n * rows - size), SUB)
    per = size // pieces
    copies = [
        pltpu.make_async_copy(
            moving.at[pl.ds(pl.multiple_of(base + i * per, SUB), per), :],
            window.at[pl.ds(i * per, per), :],
            sem.at[i],
        )
        for i in range(pieces)
    ]
    for copy in copies:
        copy.start()
    for copy in copies:
        copy.wait()
    pack_band(window, base, out, band, n, rows)


def pack_kernel(n, rows, shifts, strip, *outs):
    me = lax.axis_index("tile")
    for out, k in zip(outs, shifts):
        pack_band(strip, 0, out, lax.rem(me + k, n), n, rows)


def row_sums(ref, out, rows):
    for g in range((rows + SUB) // SUB):
        y = g * SUB
        last = min(SUB, rows + 6 - y)
        out[y : y + last, :] = (
            ref[y : y + last, :] + ref[y + 1 : y + 1 + last, :] + ref[y + 2 : y + 2 + last, :]
        )

    def total(y, size):
        return out[y : y + size, :] + out[y + 3 : y + 3 + size, :] + out[y + 6 : y + 6 + size, :]

    return total


def split(x):
    high = x.astype(BF16)
    rest = x - high.astype(F32)
    middle = rest.astype(BF16)
    low = (rest - middle.astype(F32)).astype(BF16)
    return high, middle, low


def put(terms, source, y, x):
    at = pl.ds(pl.multiple_of((source + 1) * LANES, LANES), LANES)
    for t, part in enumerate(split(x)):
        terms[t, y : y + x.shape[0], at] = part


def clear_ends(terms):
    zeros = jnp.zeros((terms.shape[1], LANES), BF16)
    for t in range(3):
        terms[t, :, :LANES] = zeros
        terms[t, :, terms.shape[2] - LANES :] = zeros


def lane_sums(arrays, width, size, weights):
    wide = size + 2 * LANES
    left = [
        jnp.concatenate([terms[t, :, start : start + wide] for t in range(3)], axis=1)
        for terms in arrays
        for start in range(0, width, size)
    ]
    out = jnp.dot(jnp.concatenate(left, axis=0), weights, preferred_element_type=F32)
    rows = arrays[0].shape[1]
    parts = [out[i * rows : (i + 1) * rows] for i in range(len(left))]
    count = width // size
    return [parts[i * count : (i + 1) * count] for i in range(len(arrays))]


def band_matrix(first, last, size):
    shape = (size + 2 * LANES, size)
    source = lax.broadcasted_iota(jnp.int32, shape, 0)
    target = lax.broadcasted_iota(jnp.int32, shape, 1)
    distance = source - target - LANES
    band = jnp.where((distance >= first) & (distance <= last), 1.0, 0.0).astype(BF16)
    return jnp.concatenate([band] * 3, axis=0)


def narrow(values, bit):
    return [jnp.where(bit, values[i + 4], values[i]) for i in range(4)] + [values[4]]


def moving_kernel(n, rows, width, *refs):
    blocks, offsets, fractions = refs[:n], refs[n], refs[n + 1]
    base, linear, square, msum, mvar = refs[n + 2 : n + 7]
    image, sums, squares, shifted, sq, three, obuf, fbuf, sem = refs[n + 7 :]
    me = lax.axis_index("tile")
    copies = [
        pltpu.make_async_copy(offsets, obuf, sem.at[0]),
        pltpu.make_async_copy(fractions, fbuf, sem.at[1]),
    ]
    for copy in copies:
        copy.start()
    deep = rows + 2 * HALO
    inv = 1.0 / float((2 * RADIUS + 1) ** 2)
    for terms in (sums, squares):
        clear_ends(terms)
    for place, k in enumerate(hops(n) + [0]):
        block = blocks[place]
        source = lax.rem(me - k + n, n)
        for y in range(0, deep, 2 * SUB):
            size = min(2 * SUB, deep - y)
            x = block[y : y + size, :]
            sq[place, y : y + size, :] = x * x
            at = pl.ds(pl.multiple_of(source * LANES, LANES), LANES)
            image[y : y + size, at] = x
        for which, (ref, terms) in enumerate(((block, sums), (sq.at[place], squares))):
            total = row_sums(ref, three.at[which, place], rows)
            for y in range(0, rows, 2 * SUB):
                put(terms, source, y, total(y, 2 * SUB))
    size = LANES * (2 if n % 2 == 0 else 1)
    window = band_matrix(-RADIUS, RADIUS, size)
    totals, seconds = lane_sums((sums, squares), width, size, window)
    for place, (total, second) in enumerate(zip(totals, seconds)):
        at = pl.ds(place * size, size)
        msum[:, at] = total
        mvar[:, at] = second - total * total * inv
    image[:, width:] = jnp.zeros((deep, LANES), F32)
    for y in range(0, deep, SUB):
        x = image[y : y + SUB, :]
        for c in range(-REACH, REACH + 2):
            turned = pltpu.roll(x, (-c) % x.shape[1], 1) if c else x
            for block in range(n):
                shifted[block, c + REACH, y : y + SUB, :] = turned[
                    :, block * LANES : (block + 1) * LANES
                ]
    for copy in copies:
        copy.wait()
    span = 2 * REACH + 2

    def unit(s, y0):
        at = pl.ds(s * LANES, LANES)
        down = obuf[0, y0 : y0 + SUB, at] + REACH
        along = obuf[1, y0 : y0 + SUB, at] + REACH
        down_bits = [down >= 4, (down & 2) == 2, (down & 1) == 1]
        along_bits = [along >= 4, (along & 2) == 2, (along & 1) == 1]

        def load(r):
            e = y0 + r + HALO - REACH
            return [shifted[s, c, e : e + SUB, :] for c in range(span)]

        grid = []
        for r in range(5):
            line = load(r)
            if r < 4:
                line = [jnp.where(down_bits[0], b, a) for a, b in zip(line, load(r + 4))]
            grid.append(narrow(line, along_bits[0]))
        for place, step in ((1, 2), (2, 1)):
            across_bit, down_bit = along_bits[place], down_bits[place]
            lines = [
                [jnp.where(down_bit, b, a) for a, b in zip(grid[r], grid[r + step])]
                for r in range(step + 1)
            ]
            grid = [
                [jnp.where(across_bit, line[i + step], line[i]) for i in range(step + 1)]
                for line in lines
            ]
        (top_left, top_right), (bottom_left, bottom_right) = grid
        rf = fbuf[0, y0 : y0 + SUB, at]
        cf = fbuf[1, y0 : y0 + SUB, at]
        across = top_right - top_left
        base[y0 : y0 + SUB, at] = top_left
        linear[y0 : y0 + SUB, at] = cf * across + rf * (bottom_left - top_left)
        square[y0 : y0 + SUB, at] = (rf * cf) * ((bottom_right - bottom_left) - across)

    for s in range(n):
        for g in range(rows // SUB):
            unit(s, g * SUB)


def final_kernel(n, rows, width, *refs):
    fixed, moving = refs[:n], refs[n : 2 * n]
    base, linear, square, msum, mvar, out = refs[2 * n : 2 * n + 6]
    sums, squares, crosses, ff, fm, three, obuf, sem = refs[2 * n + 6 :]
    me = lax.axis_index("tile")
    inv = 1.0 / float((2 * RADIUS + 1) ** 2)
    for terms in (sums, squares, crosses):
        clear_ends(terms)
    for place, k in enumerate(hops(n) + [0]):
        f, m = fixed[place], moving[place]
        source = lax.rem(me - k + n, n)
        for y in range(0, rows + 2 * HALO, SUB):
            x = f[y : y + SUB, :]
            ff[place, y : y + SUB, :] = x * x
            fm[place, y : y + SUB, :] = x * m[y : y + SUB, :]
        for which, (ref, terms) in enumerate(
            ((f, sums), (ff.at[place], squares), (fm.at[place], crosses))
        ):
            total = row_sums(ref, three.at[which, place], rows)
            for y in range(0, rows, 2 * SUB):
                put(terms, source, y, total(y, 2 * SUB))
    size = LANES * (2 if n % 2 == 0 else 1)
    window = band_matrix(-RADIUS, RADIUS, size)
    copies = []
    windows = lane_sums((sums, squares, crosses), width, size, window)
    for place, (fsum, second, cross) in enumerate(zip(*windows)):
        at = pl.ds(place * size, size)
        fvar = second - fsum * fsum * inv
        cov = cross - fsum * msum[:, at] * inv
        conf = 0.5 + 0.5 * (cov * lax.rsqrt(fvar * mvar[:, at] + 0.001))
        obuf[:, at] = base[:, at] + conf * (linear[:, at] + conf * square[:, at])
        copy = pltpu.make_async_copy(obuf.at[:, at], out.at[:, at], sem.at[place])
        copy.start()
        copies.append(copy)
    for copy in copies:
        copy.wait()


VMEM = pl.BlockSpec(memory_space=pltpu.VMEM)
ANY = pl.BlockSpec(memory_space=pl.ANY)


def held(shape):
    return pltpu.VMEM(shape, F32)


def near(x):
    return pltpu.with_memory_space_constraint(x, pltpu.VMEM)


def far(x):
    return pltpu.with_memory_space_constraint(x, pltpu.HBM)


def on_device(n, fixed, moving, offsets, fractions):
    rows, width = offsets.shape[1:]
    strip = moving.shape
    deep = rows + 2 * HALO
    band = held((deep, strip[1]))
    plane = held((rows, width))
    params = pltpu.CompilerParams(vmem_limit_bytes=ROOM)
    pieces = 3
    first = pl.pallas_call(
        functools.partial(first_kernel, n, rows, pieces),
        out_shape=band,
        in_specs=[ANY],
        out_specs=VMEM,
        scratch_shapes=[
            pltpu.VMEM((rows + 2 * SUB, strip[1]), F32),
            pltpu.SemaphoreType.DMA((pieces,)),
        ],
        compiler_params=params,
        name="first",
    )(far(moving))
    order = hops(n)

    def pack(image, shifts):
        return pl.pallas_call(
            functools.partial(pack_kernel, n, rows, shifts),
            out_shape=[band] * len(shifts),
            in_specs=[VMEM],
            out_specs=[VMEM] * len(shifts),
            compiler_params=params,
            name="pack",
        )(near(image))

    def send(blocks):
        got = [
            lax.ppermute(block, "tile", [(i, (i + k) % n) for i in range(n)])
            for block, k in zip(blocks, order)
        ]
        return got + [blocks[-1]]

    moved = send([first, *pack(moving, order[1:] + [0])])
    fixes = send(pack(fixed, order + [0]))
    parts = pl.pallas_call(
        functools.partial(moving_kernel, n, rows, width),
        out_shape=[plane] * 5,
        in_specs=[VMEM] * n + [ANY] * 2,
        out_specs=[VMEM] * 5,
        scratch_shapes=[
            pltpu.VMEM((deep, width + LANES), F32),
            pltpu.VMEM((3, rows, width + 2 * LANES), BF16),
            pltpu.VMEM((3, rows, width + 2 * LANES), BF16),
            pltpu.VMEM((n, 2 * REACH + 2, deep, LANES), F32),
            pltpu.VMEM((n, deep, LANES), F32),
            pltpu.VMEM((2, n, deep, LANES), F32),
            pltpu.VMEM(offsets.shape, jnp.int32),
            pltpu.VMEM(fractions.shape, F32),
            pltpu.SemaphoreType.DMA((2,)),
        ],
        compiler_params=pltpu.CompilerParams(vmem_limit_bytes=ROOM),
        cost_estimate=pl.CostEstimate(
            flops=200 * rows * width, bytes_accessed=16 * rows * width, transcendentals=0
        ),
        name="moving_part",
    )(*map(near, moved), far(offsets), far(fractions))
    return pl.pallas_call(
        functools.partial(final_kernel, n, rows, width),
        out_shape=jax.ShapeDtypeStruct((rows, width), F32),
        in_specs=[VMEM] * (2 * n + 5),
        out_specs=ANY,
        scratch_shapes=[
            pltpu.VMEM((3, rows, width + 2 * LANES), BF16),
            pltpu.VMEM((3, rows, width + 2 * LANES), BF16),
            pltpu.VMEM((3, rows, width + 2 * LANES), BF16),
            pltpu.VMEM((n, deep, LANES), F32),
            pltpu.VMEM((n, deep, LANES), F32),
            pltpu.VMEM((3, n, deep, LANES), F32),
            pltpu.VMEM((rows, width), F32),
            pltpu.SemaphoreType.DMA((n,)),
        ],
        compiler_params=pltpu.CompilerParams(vmem_limit_bytes=ROOM),
        name="final_part",
    )(*map(near, (*fixes, *moved, *parts)))


def solution(mesh):
    placed = (
        P("pair", "tile"),
        P("pair", "tile"),
        P(None, ("pair", "tile"), None),
        P(None, ("pair", "tile"), None),
    )
    return jax.shard_map(
        functools.partial(on_device, mesh.shape["tile"]),
        mesh=mesh,
        in_specs=placed,
        out_specs=P(("pair", "tile"), None),
        check_vma=False,
    )
```

```python
import functools

import jax
import jax.numpy as jnp
from jax import lax
from jax.experimental import pallas as pl
from jax.experimental.pallas import tpu as pltpu
from jax.sharding import PartitionSpec as P

RADIUS = 4
REACH = 3
HALO = max(RADIUS, REACH + 1)
LANES = 128
SUB = 8
F32 = jnp.float32
BF16 = jnp.bfloat16
ROOM = 28 * 2**20


def hops(n):
    middle = n // 2
    return [middle] + [k for k in range(1, n) if k != middle]


def pack_band(strip, base, out, band, n, rows):
    start = pl.multiple_of(band * rows - base, SUB)
    size = strip.shape[0]
    top = strip[pl.ds(pl.multiple_of(jnp.maximum(start - SUB, 0), SUB), SUB), :]
    out[0:HALO, :] = jnp.where(band > 0, top, 0.0)[SUB - HALO :, :]
    out[HALO : HALO + rows, :] = strip[pl.ds(start, rows), :]
    low = strip[pl.ds(pl.multiple_of(jnp.minimum(start + rows, size - SUB), SUB), SUB), :]
    out[HALO + rows :, :] = jnp.where(band < n - 1, low, 0.0)[:HALO, :]


def first_kernel(n, rows, pieces, moving, out, window, sem):
    band = lax.rem(lax.axis_index("tile") + hops(n)[0], n)
    size = window.shape[0]
    base = pl.multiple_of(jnp.clip(band * rows - SUB, 0, n * rows - size), SUB)
    per = size // pieces
    copies = [
        pltpu.make_async_copy(
            moving.at[pl.ds(pl.multiple_of(base + i * per, SUB), per), :],
            window.at[pl.ds(i * per, per), :],
            sem.at[i],
        )
        for i in range(pieces)
    ]
    for copy in copies:
        copy.start()
    for copy in copies:
        copy.wait()
    pack_band(window, base, out, band, n, rows)


def pack_kernel(n, rows, shifts, strip, *outs):
    me = lax.axis_index("tile")
    for out, k in zip(outs, shifts):
        pack_band(strip, 0, out, lax.rem(me + k, n), n, rows)


def row_sums(ref, out, rows):
    for g in range((rows + SUB) // SUB):
        y = g * SUB
        last = min(SUB, rows + 6 - y)
        out[y : y + last, :] = (
            ref[y : y + last, :] + ref[y + 1 : y + 1 + last, :] + ref[y + 2 : y + 2 + last, :]
        )

    def total(y, size):
        return out[y : y + size, :] + out[y + 3 : y + 3 + size, :] + out[y + 6 : y + 6 + size, :]

    return total


def split(x):
    high = x.astype(BF16)
    rest = x - high.astype(F32)
    middle = rest.astype(BF16)
    low = (rest - middle.astype(F32)).astype(BF16)
    return high, middle, low


def put(terms, source, y, x):
    at = pl.ds(pl.multiple_of((source + 1) * LANES, LANES), LANES)
    for t, part in enumerate(split(x)):
        terms[t, y : y + x.shape[0], at] = part


def clear_ends(terms):
    zeros = jnp.zeros((terms.shape[1], LANES), BF16)
    for t in range(3):
        terms[t, :, :LANES] = zeros
        terms[t, :, terms.shape[2] - LANES :] = zeros


def lane_sums(arrays, width, size, weights):
    wide = size + 2 * LANES
    left = [
        jnp.concatenate([terms[t, :, start : start + wide] for t in range(3)], axis=1)
        for terms in arrays
        for start in range(0, width, size)
    ]
    out = jnp.dot(jnp.concatenate(left, axis=0), weights, preferred_element_type=F32)
    rows = arrays[0].shape[1]
    parts = [out[i * rows : (i + 1) * rows] for i in range(len(left))]
    count = width // size
    return [parts[i * count : (i + 1) * count] for i in range(len(arrays))]


def band_matrix(first, last, size):
    shape = (size + 2 * LANES, size)
    source = lax.broadcasted_iota(jnp.int32, shape, 0)
    target = lax.broadcasted_iota(jnp.int32, shape, 1)
    distance = source - target - LANES
    band = jnp.where((distance >= first) & (distance <= last), 1.0, 0.0).astype(BF16)
    return jnp.concatenate([band] * 3, axis=0)


def narrow(values, bit):
    return [jnp.where(bit, values[i + 4], values[i]) for i in range(4)] + [values[4]]


def fixed_row_sums(f, m, products, rows):
    for y in range(0, f.shape[0], SUB):
        x = f[y : y + SUB, :]
        products[0, y : y + SUB, :] = x * x
        products[1, y : y + SUB, :] = x * m[y : y + SUB, :]
    return [
        row_sums(ref, products.at[2 + which], rows)
        for which, ref in enumerate((f, products.at[0], products.at[1]))
    ]


def lane_windows(terms, out):
    arrays, _, rows, width = terms.shape
    blocks = width // LANES
    size = LANES * (2 if blocks % 2 == 0 else 1)
    source = lax.broadcasted_iota(jnp.int32, (size, size), 0)
    target = lax.broadcasted_iota(jnp.int32, (size, size), 1)
    near_by = (source - target <= RADIUS) & (target - source <= RADIUS)
    inside = jnp.where(near_by, 1.0, 0.0).astype(BF16)
    source = lax.broadcasted_iota(jnp.int32, (2 * LANES, 2 * LANES), 0)
    target = lax.broadcasted_iota(jnp.int32, (2 * LANES, 2 * LANES), 1)
    near_by = (source - target <= RADIUS) & (target - source <= RADIUS)
    other = (source < LANES) != (target < LANES)
    across = jnp.where(near_by & other, 1.0, 0.0).astype(BF16)

    def times(starts, wide, weights):
        left = [
            jnp.concatenate([terms[a, t, :, start : start + wide] for t in range(3)], axis=1)
            for a in range(arrays)
            for start in starts
        ]
        got = jnp.dot(
            jnp.concatenate(left, axis=0),
            jnp.concatenate([weights] * 3, axis=0),
            preferred_element_type=F32,
        )
        for i in range(len(left)):
            yield divmod(i, len(starts)), got[i * rows : (i + 1) * rows]

    starts = list(range(0, width, size))
    for (a, place), part in times(starts, size, inside):
        out[a, :, starts[place] : starts[place] + size] = part
    starts = [start - LANES for start in starts[1:]]
    if starts:
        for (a, place), part in times(starts, 2 * LANES, across):
            at = slice(starts[place], starts[place] + 2 * LANES)
            out[a, :, at] = out[a, :, at] + part


def moving_kernel(n, rows, width, *refs):
    blocks, fixed, offsets, fractions = refs[:n], refs[n], refs[n + 1], refs[n + 2]
    base, linear, square, msum, mvar, own = refs[n + 3 : n + 9]
    image, sums, squares, shifted, sq, three, products, obuf, fbuf, sem = refs[n + 9 :]
    me = lax.axis_index("tile")
    copies = [
        pltpu.make_async_copy(offsets, obuf, sem.at[0]),
        pltpu.make_async_copy(fractions, fbuf, sem.at[1]),
    ]
    for copy in copies:
        copy.start()
    for which, total in enumerate(fixed_row_sums(fixed, blocks[n - 1], products, rows)):
        own[which] = total(0, rows)
    deep = rows + 2 * HALO
    inv = 1.0 / float((2 * RADIUS + 1) ** 2)
    for terms in (sums, squares):
        clear_ends(terms)
    for place, k in enumerate(hops(n) + [0]):
        block = blocks[place]
        source = lax.rem(me - k + n, n)
        for y in range(0, deep, 2 * SUB):
            size = min(2 * SUB, deep - y)
            x = block[y : y + size, :]
            sq[place, y : y + size, :] = x * x
            at = pl.ds(pl.multiple_of(source * LANES, LANES), LANES)
            image[y : y + size, at] = x
        for which, (ref, terms) in enumerate(((block, sums), (sq.at[place], squares))):
            total = row_sums(ref, three.at[which, place], rows)
            for y in range(0, rows, 2 * SUB):
                put(terms, source, y, total(y, 2 * SUB))
    size = LANES * (2 if n % 2 == 0 else 1)
    window = band_matrix(-RADIUS, RADIUS, size)
    totals, seconds = lane_sums((sums, squares), width, size, window)
    for place, (total, second) in enumerate(zip(totals, seconds)):
        at = pl.ds(place * size, size)
        msum[:, at] = total
        mvar[:, at] = second - total * total * inv
    image[:, width:] = jnp.zeros((deep, LANES), F32)
    for y in range(0, deep, SUB):
        x = image[y : y + SUB, :]
        for c in range(-REACH, REACH + 2):
            turned = pltpu.roll(x, (-c) % x.shape[1], 1) if c else x
            for block in range(n):
                shifted[block, c + REACH, y : y + SUB, :] = turned[
                    :, block * LANES : (block + 1) * LANES
                ]
    for copy in copies:
        copy.wait()
    span = 2 * REACH + 2

    def unit(s, y0):
        at = pl.ds(s * LANES, LANES)
        down = obuf[0, y0 : y0 + SUB, at] + REACH
        along = obuf[1, y0 : y0 + SUB, at] + REACH
        down_bits = [down >= 4, (down & 2) == 2, (down & 1) == 1]
        along_bits = [along >= 4, (along & 2) == 2, (along & 1) == 1]

        def load(r):
            e = y0 + r + HALO - REACH
            return [shifted[s, c, e : e + SUB, :] for c in range(span)]

        grid = []
        for r in range(5):
            line = load(r)
            if r < 4:
                line = [jnp.where(down_bits[0], b, a) for a, b in zip(line, load(r + 4))]
            grid.append(narrow(line, along_bits[0]))
        for place, step in ((1, 2), (2, 1)):
            across_bit, down_bit = along_bits[place], down_bits[place]
            lines = [
                [jnp.where(down_bit, b, a) for a, b in zip(grid[r], grid[r + step])]
                for r in range(step + 1)
            ]
            grid = [
                [jnp.where(across_bit, line[i + step], line[i]) for i in range(step + 1)]
                for line in lines
            ]
        (top_left, top_right), (bottom_left, bottom_right) = grid
        rf = fbuf[0, y0 : y0 + SUB, at]
        cf = fbuf[1, y0 : y0 + SUB, at]
        across = top_right - top_left
        base[y0 : y0 + SUB, at] = top_left
        linear[y0 : y0 + SUB, at] = cf * across + rf * (bottom_left - top_left)
        square[y0 : y0 + SUB, at] = (rf * cf) * ((bottom_right - bottom_left) - across)

    for s in range(n):
        for g in range(rows // SUB):
            unit(s, g * SUB)


def final_kernel(n, rows, width, chunks, *refs):
    fixed, moving = refs[: n - 1], refs[n - 1 : 2 * n - 2]
    base, linear, square, msum, mvar, own, out = refs[2 * n - 2 : 2 * n + 5]
    summed, triple, terms, windows, products, obuf, sem = refs[2 * n + 5 :]
    me = lax.axis_index("tile")
    inv = 1.0 / float((2 * RADIUS + 1) ** 2)
    extent = width + LANES
    summed[:, width:] = jnp.zeros((rows, LANES), F32)

    def keep(source, totals):
        at = pl.ds(pl.multiple_of(source * LANES, LANES), LANES)
        for y in range(0, rows, 2 * SUB):
            summed[y : y + 2 * SUB, at] = totals[0](y, 2 * SUB)
            for which in range(2):
                for t, part in enumerate(split(totals[1 + which](y, 2 * SUB))):
                    terms[which, t, y : y + 2 * SUB, at] = part

    keep(me, [lambda y, size, w=w: own[w, y : y + size, :] for w in range(3)])
    for place, k in enumerate(hops(n)):
        keep(
            lax.rem(me - k + n, n),
            fixed_row_sums(fixed[place], moving[place], products.at[place], rows),
        )
    lane_windows(terms, windows)
    for y in range(0, rows, SUB):
        x = summed[y : y + SUB, :]
        triple[y : y + SUB, :] = x + pltpu.roll(x, 1, 1) + pltpu.roll(x, extent - 1, 1)
    per = rows // chunks
    copies = []
    for chunk in range(chunks):
        for y in range(chunk * per, (chunk + 1) * per, SUB):
            at = slice(y, y + SUB)
            x = triple[at, :]
            fsum = (x + pltpu.roll(x, 3, 1) + pltpu.roll(x, extent - 3, 1))[:, :width]
            fvar = windows[0, at, :] - fsum * fsum * inv
            cov = windows[1, at, :] - fsum * msum[at, :] * inv
            conf = 0.5 + 0.5 * (cov * lax.rsqrt(fvar * mvar[at, :] + 0.001))
            obuf[at, :] = base[at, :] + conf * (linear[at, :] + conf * square[at, :])
        span = pl.ds(chunk * per, per)
        copy = pltpu.make_async_copy(obuf.at[span, :], out.at[span, :], sem.at[chunk])
        copy.start()
        copies.append(copy)
    for copy in copies:
        copy.wait()


VMEM = pl.BlockSpec(memory_space=pltpu.VMEM)
ANY = pl.BlockSpec(memory_space=pl.ANY)


def held(shape):
    return pltpu.VMEM(shape, F32)


def near(x):
    return pltpu.with_memory_space_constraint(x, pltpu.VMEM)


def far(x):
    return pltpu.with_memory_space_constraint(x, pltpu.HBM)


def on_device(n, fixed, moving, offsets, fractions):
    rows, width = offsets.shape[1:]
    strip = moving.shape
    deep = rows + 2 * HALO
    band = held((deep, strip[1]))
    plane = held((rows, width))
    params = pltpu.CompilerParams(vmem_limit_bytes=ROOM)
    pieces = 3
    first = pl.pallas_call(
        functools.partial(first_kernel, n, rows, pieces),
        out_shape=band,
        in_specs=[ANY],
        out_specs=VMEM,
        scratch_shapes=[
            pltpu.VMEM((rows + 2 * SUB, strip[1]), F32),
            pltpu.SemaphoreType.DMA((pieces,)),
        ],
        compiler_params=params,
        name="first",
    )(far(moving))
    order = hops(n)

    def pack(image, shifts):
        return pl.pallas_call(
            functools.partial(pack_kernel, n, rows, shifts),
            out_shape=[band] * len(shifts),
            in_specs=[VMEM],
            out_specs=[VMEM] * len(shifts),
            compiler_params=params,
            name="pack",
        )(near(image))

    def send(blocks):
        got = [
            lax.ppermute(block, "tile", [(i, (i + k) % n) for i in range(n)])
            for block, k in zip(blocks, order)
        ]
        return got + [blocks[-1]]

    moved = send([first, *pack(moving, order[1:] + [0])])
    fixes = send(pack(fixed, order + [0]))
    parts = pl.pallas_call(
        functools.partial(moving_kernel, n, rows, width),
        out_shape=[plane] * 5 + [held((3, rows, strip[1]))],
        in_specs=[VMEM] * (n + 1) + [ANY] * 2,
        out_specs=[VMEM] * 6,
        scratch_shapes=[
            pltpu.VMEM((deep, width + LANES), F32),
            pltpu.VMEM((3, rows, width + 2 * LANES), BF16),
            pltpu.VMEM((3, rows, width + 2 * LANES), BF16),
            pltpu.VMEM((n, 2 * REACH + 2, deep, LANES), F32),
            pltpu.VMEM((n, deep, LANES), F32),
            pltpu.VMEM((2, n, deep, LANES), F32),
            pltpu.VMEM((5, deep, LANES), F32),
            pltpu.VMEM(offsets.shape, jnp.int32),
            pltpu.VMEM(fractions.shape, F32),
            pltpu.SemaphoreType.DMA((2,)),
        ],
        compiler_params=params,
        cost_estimate=pl.CostEstimate(
            flops=200 * rows * width, bytes_accessed=16 * rows * width, transcendentals=0
        ),
        name="moving_part",
    )(*map(near, (*moved, fixes[-1])), far(offsets), far(fractions))
    chunks = 4
    return pl.pallas_call(
        functools.partial(final_kernel, n, rows, width, chunks),
        out_shape=jax.ShapeDtypeStruct((rows, width), F32),
        in_specs=[VMEM] * (2 * n + 4),
        out_specs=ANY,
        scratch_shapes=[
            pltpu.VMEM((rows, width + LANES), F32),
            pltpu.VMEM((rows, width + LANES), F32),
            pltpu.VMEM((2, 3, rows, width), BF16),
            pltpu.VMEM((2, rows, width), F32),
            pltpu.VMEM((n - 1, 5, deep, LANES), F32),
            pltpu.VMEM((rows, width), F32),
            pltpu.SemaphoreType.DMA((chunks,)),
        ],
        compiler_params=params,
        name="final_part",
    )(*map(near, (*fixes[:-1], *moved[:-1], *parts)))


def solution(mesh):
    placed = (
        P("pair", "tile"),
        P("pair", "tile"),
        P(None, ("pair", "tile"), None),
        P(None, ("pair", "tile"), None),
    )
    return jax.shard_map(
        functools.partial(on_device, mesh.shape["tile"]),
        mesh=mesh,
        in_specs=placed,
        out_specs=P(("pair", "tile"), None),
        check_vma=False,
    )
```

```python
import functools

import jax
import jax.numpy as jnp
from jax import lax
from jax.experimental import pallas as pl
from jax.experimental.pallas import tpu as pltpu
from jax.sharding import PartitionSpec as P

RADIUS = 4
REACH = 3
HALO = max(RADIUS, REACH + 1)
LANES = 128
SUB = 8
F32 = jnp.float32
BF16 = jnp.bfloat16
ROOM = 28 * 2**20


PIECES = 3
STEPS = 2
MOVING_ORDER = (2, 1, 3)
FIXED_ORDER = (2, 1, 3)


def hops(n, first=(2, 1, 3)):
    return list(first) if n == 4 else list(range(1, n))


def pack_band(strip, base, out, band, n, rows):
    start = pl.multiple_of(band * rows - base, SUB)
    size = strip.shape[0]
    top = strip[pl.ds(pl.multiple_of(jnp.maximum(start - SUB, 0), SUB), SUB), :]
    out[0:HALO, :] = jnp.where(band > 0, top, 0.0)[SUB - HALO :, :]
    out[HALO : HALO + rows, :] = strip[pl.ds(start, rows), :]
    low = strip[pl.ds(pl.multiple_of(jnp.minimum(start + rows, size - SUB), SUB), SUB), :]
    out[HALO + rows :, :] = jnp.where(band < n - 1, low, 0.0)[:HALO, :]


def first_kernel(n, rows, pieces, moving, out, window, sem):
    band = lax.rem(lax.axis_index("tile") + hops(n, MOVING_ORDER)[0], n)
    size = window.shape[0]
    base = pl.multiple_of(jnp.clip(band * rows - SUB, 0, n * rows - size), SUB)
    per = size // pieces
    copies = [
        pltpu.make_async_copy(
            moving.at[pl.ds(pl.multiple_of(base + i * per, SUB), per), :],
            window.at[pl.ds(i * per, per), :],
            sem.at[i],
        )
        for i in range(pieces)
    ]
    for copy in copies:
        copy.start()
    for copy in copies:
        copy.wait()
    pack_band(window, base, out, band, n, rows)


def pack_kernel(n, rows, shifts, strip, *outs):
    me = lax.axis_index("tile")
    for out, k in zip(outs, shifts):
        pack_band(strip, 0, out, lax.rem(me + k, n), n, rows)


def row_sums(ref, out, rows):
    for g in range((rows + SUB) // SUB):
        y = g * SUB
        last = min(SUB, rows + 6 - y)
        out[y : y + last, :] = (
            ref[y : y + last, :] + ref[y + 1 : y + 1 + last, :] + ref[y + 2 : y + 2 + last, :]
        )

    def total(y, size):
        return out[y : y + size, :] + out[y + 3 : y + 3 + size, :] + out[y + 6 : y + 6 + size, :]

    return total


def split(x):
    high = x.astype(BF16)
    rest = x - high.astype(F32)
    middle = rest.astype(BF16)
    low = (rest - middle.astype(F32)).astype(BF16)
    return high, middle, low


def put(terms, source, y, x):
    at = pl.ds(pl.multiple_of((source + 1) * LANES, LANES), LANES)
    for t, part in enumerate(split(x)):
        terms[t, y : y + x.shape[0], at] = part


def clear_ends(terms):
    zeros = jnp.zeros((terms.shape[1], LANES), BF16)
    for t in range(3):
        terms[t, :, :LANES] = zeros
        terms[t, :, terms.shape[2] - LANES :] = zeros


def lane_sums(arrays, width, size, weights):
    wide = size + 2 * LANES
    left = [
        jnp.concatenate([terms[t, :, start : start + wide] for t in range(3)], axis=1)
        for terms in arrays
        for start in range(0, width, size)
    ]
    out = jnp.dot(jnp.concatenate(left, axis=0), weights, preferred_element_type=F32)
    rows = arrays[0].shape[1]
    parts = [out[i * rows : (i + 1) * rows] for i in range(len(left))]
    count = width // size
    return [parts[i * count : (i + 1) * count] for i in range(len(arrays))]


def band_matrix(first, last, size):
    shape = (size + 2 * LANES, size)
    source = lax.broadcasted_iota(jnp.int32, shape, 0)
    target = lax.broadcasted_iota(jnp.int32, shape, 1)
    distance = source - target - LANES
    band = jnp.where((distance >= first) & (distance <= last), 1.0, 0.0).astype(BF16)
    return jnp.concatenate([band] * 3, axis=0)


def narrow(values, bit):
    return [jnp.where(bit, values[i + 4], values[i]) for i in range(4)] + [values[4]]


def fixed_row_sums(f, m, products, rows):
    for y in range(0, f.shape[0], SUB):
        x = f[y : y + SUB, :]
        products[0, y : y + SUB, :] = x * x
        products[1, y : y + SUB, :] = x * m[y : y + SUB, :]
    return [
        row_sums(ref, products.at[2 + which], rows)
        for which, ref in enumerate((f, products.at[0], products.at[1]))
    ]


def lane_windows(terms, out):
    _, rows, width = terms.shape
    blocks = width // LANES
    size = LANES * (2 if blocks % 2 == 0 else 1)
    source = lax.broadcasted_iota(jnp.int32, (size, size), 0)
    target = lax.broadcasted_iota(jnp.int32, (size, size), 1)
    near_by = (source - target <= RADIUS) & (target - source <= RADIUS)
    inside = jnp.where(near_by, 1.0, 0.0).astype(BF16)
    source = lax.broadcasted_iota(jnp.int32, (2 * LANES, 2 * LANES), 0)
    target = lax.broadcasted_iota(jnp.int32, (2 * LANES, 2 * LANES), 1)
    near_by = (source - target <= RADIUS) & (target - source <= RADIUS)
    other = (source < LANES) != (target < LANES)
    across = jnp.where(near_by & other, 1.0, 0.0).astype(BF16)

    def times(starts, wide, weights):
        left = [
            jnp.concatenate([terms[t, :, start : start + wide] for t in range(3)], axis=1)
            for start in starts
        ]
        got = jnp.dot(
            jnp.concatenate(left, axis=0),
            jnp.concatenate([weights] * 3, axis=0),
            preferred_element_type=F32,
        )
        return [got[i * rows : (i + 1) * rows] for i in range(len(left))]

    starts = list(range(0, width, size))
    for start, part in zip(starts, times(starts, size, inside)):
        out[:, start : start + size] = part
    starts = [start - LANES for start in starts[1:]]
    if starts:
        for start, part in zip(starts, times(starts, 2 * LANES, across)):
            at = slice(start, start + 2 * LANES)
            out[:, at] = out[:, at] + part


def moving_kernel(n, rows, width, *refs):
    blocks, fixed, offsets, fractions = refs[:n], refs[n], refs[n + 1], refs[n + 2]
    base, linear, square, msum, mvar, own = refs[n + 3 : n + 9]
    image, sums, squares, shifted, sq, three, products, obuf, fbuf, sem = refs[n + 9 :]
    me = lax.axis_index("tile")
    copies = [
        pltpu.make_async_copy(offsets, obuf, sem.at[0]),
        pltpu.make_async_copy(fractions, fbuf, sem.at[1]),
    ]
    for copy in copies:
        copy.start()
    for which, total in enumerate(fixed_row_sums(fixed, blocks[n - 1], products, rows)):
        own[which] = total(0, rows)
    deep = rows + 2 * HALO
    inv = 1.0 / float((2 * RADIUS + 1) ** 2)
    for terms in (sums, squares):
        clear_ends(terms)
    for place, k in enumerate(hops(n, MOVING_ORDER) + [0]):
        block = blocks[place]
        source = lax.rem(me - k + n, n)
        for y in range(0, deep, 2 * SUB):
            size = min(2 * SUB, deep - y)
            x = block[y : y + size, :]
            sq[place, y : y + size, :] = x * x
            at = pl.ds(pl.multiple_of(source * LANES, LANES), LANES)
            image[y : y + size, at] = x
        for which, (ref, terms) in enumerate(((block, sums), (sq.at[place], squares))):
            total = row_sums(ref, three.at[which, place], rows)
            for y in range(0, rows, 2 * SUB):
                put(terms, source, y, total(y, 2 * SUB))
    size = LANES * (2 if n % 2 == 0 else 1)
    window = band_matrix(-RADIUS, RADIUS, size)
    totals, seconds = lane_sums((sums, squares), width, size, window)
    for place, (total, second) in enumerate(zip(totals, seconds)):
        at = pl.ds(place * size, size)
        msum[:, at] = total
        mvar[:, at] = second - total * total * inv
    image[:, width:] = jnp.zeros((deep, LANES), F32)
    for y in range(0, deep, SUB):
        x = image[y : y + SUB, :]
        for c in range(-REACH, REACH + 2):
            turned = pltpu.roll(x, (-c) % x.shape[1], 1) if c else x
            for block in range(n):
                shifted[block, c + REACH, y : y + SUB, :] = turned[
                    :, block * LANES : (block + 1) * LANES
                ]
    span = 2 * REACH + 2

    def unit(s, y0):
        at = pl.ds(s * LANES, LANES)
        down = obuf[0, y0 : y0 + SUB, at] + REACH
        along = obuf[1, y0 : y0 + SUB, at] + REACH
        down_bits = [down >= 4, (down & 2) == 2, (down & 1) == 1]
        along_bits = [along >= 4, (along & 2) == 2, (along & 1) == 1]

        def load(r):
            e = y0 + r + HALO - REACH
            return [shifted[s, c, e : e + SUB, :] for c in range(span)]

        grid = []
        for r in range(5):
            line = load(r)
            if r < 4:
                line = [jnp.where(down_bits[0], b, a) for a, b in zip(line, load(r + 4))]
            grid.append(narrow(line, along_bits[0]))
        for place, step in ((1, 2), (2, 1)):
            across_bit, down_bit = along_bits[place], down_bits[place]
            lines = [
                [jnp.where(down_bit, b, a) for a, b in zip(grid[r], grid[r + step])]
                for r in range(step + 1)
            ]
            grid = [
                [jnp.where(across_bit, line[i + step], line[i]) for i in range(step + 1)]
                for line in lines
            ]
        (top_left, top_right), (bottom_left, bottom_right) = grid
        rf = fbuf[0, y0 : y0 + SUB, at]
        cf = fbuf[1, y0 : y0 + SUB, at]
        across = top_right - top_left
        base[y0 : y0 + SUB, at] = top_left
        linear[y0 : y0 + SUB, at] = cf * across + rf * (bottom_left - top_left)
        square[y0 : y0 + SUB, at] = (rf * cf) * ((bottom_right - bottom_left) - across)

    for copy in copies:
        copy.wait()
    for s in range(n):
        for g in range(rows // SUB):
            unit(s, g * SUB)


def final_kernel(n, rows, width, *refs):
    per = rows // STEPS
    sem = refs[-1]

    def result(step):
        at = pl.ds(pl.multiple_of(step * per, SUB), per)
        obuf, out = refs[-2], refs[2 * n + 4]
        return pltpu.make_async_copy(obuf.at[at, :], out.at[at, :], sem.at[step])

    def one(step, carry):
        final_rows(n, per, width, pl.multiple_of(step * per, SUB), refs)
        result(step).start()
        return carry

    lax.fori_loop(0, STEPS, one, 0)
    for step in range(STEPS):
        result(step).wait()


def final_rows(n, rows, width, start, refs):
    deep = pl.ds(start, rows + 2 * HALO)
    here = pl.ds(start, rows)
    fixed = [ref.at[deep, :] for ref in refs[: n - 1]]
    moving = [ref.at[deep, :] for ref in refs[n - 1 : 2 * n - 2]]
    base, linear, square, msum, mvar = [ref.at[here, :] for ref in refs[2 * n - 2 : 2 * n + 3]]
    own = refs[2 * n + 3].at[:, here, :]
    summed, triple, square_terms, cross_terms, windows, products, obuf = refs[2 * n + 5 : -1]
    obuf = obuf.at[here, :]
    me = lax.axis_index("tile")
    inv = 1.0 / float((2 * RADIUS + 1) ** 2)
    extent = width + LANES
    summed[:, width:] = jnp.zeros((rows, LANES), F32)
    blocks = [(me, [lambda y, size, w=w: own[w, y : y + size, :] for w in range(3)])]
    for place, k in enumerate(hops(n, FIXED_ORDER)):
        totals = fixed_row_sums(fixed[place], moving[place], products.at[place], rows)
        blocks.append((lax.rem(me - k + n, n), totals))

    def places():
        for source, totals in blocks:
            yield pl.ds(pl.multiple_of(source * LANES, LANES), LANES), totals

    for at, totals in places():
        for y in range(0, rows, SUB):
            summed[y : y + SUB, at] = totals[0](y, SUB)
    for y in range(0, rows, SUB):
        x = summed[y : y + SUB, :]
        triple[y : y + SUB, :] = x + pltpu.roll(x, 1, 1) + pltpu.roll(x, extent - 1, 1)
    for which, terms in enumerate((square_terms, cross_terms)):
        for at, totals in places():
            for y in range(0, rows, 2 * SUB):
                for t, part in enumerate(split(totals[1 + which](y, 2 * SUB))):
                    terms[t, y : y + 2 * SUB, at] = part
        lane_windows(terms, windows.at[which])
    for y in range(0, rows, SUB):
        at = slice(y, y + SUB)
        x = triple[at, :]
        fsum = (x + pltpu.roll(x, 3, 1) + pltpu.roll(x, extent - 3, 1))[:, :width]
        fvar = windows[0, at, :] - fsum * fsum * inv
        cov = windows[1, at, :] - fsum * msum[at, :] * inv
        conf = 0.5 + 0.5 * (cov * lax.rsqrt(fvar * mvar[at, :] + 0.001))
        obuf[at, :] = base[at, :] + conf * (linear[at, :] + conf * square[at, :])


VMEM = pl.BlockSpec(memory_space=pltpu.VMEM)
ANY = pl.BlockSpec(memory_space=pl.ANY)


def held(shape):
    return pltpu.VMEM(shape, F32)


def near(x):
    return pltpu.with_memory_space_constraint(x, pltpu.VMEM)


def far(x):
    return pltpu.with_memory_space_constraint(x, pltpu.HBM)


def on_device(n, fixed, moving, offsets, fractions):
    rows, width = offsets.shape[1:]
    strip = moving.shape
    deep = rows + 2 * HALO
    band = held((deep, strip[1]))
    plane = held((rows, width))
    params = pltpu.CompilerParams(vmem_limit_bytes=ROOM)
    pieces = PIECES
    first = pl.pallas_call(
        functools.partial(first_kernel, n, rows, pieces),
        out_shape=band,
        in_specs=[ANY],
        out_specs=VMEM,
        scratch_shapes=[
            pltpu.VMEM((rows + 2 * SUB, strip[1]), F32),
            pltpu.SemaphoreType.DMA((pieces,)),
        ],
        compiler_params=params,
        name="first",
    )(far(moving))
    order, later = hops(n, MOVING_ORDER), hops(n, FIXED_ORDER)

    def pack(image, shifts):
        return pl.pallas_call(
            functools.partial(pack_kernel, n, rows, shifts),
            out_shape=[band] * len(shifts),
            in_specs=[VMEM],
            out_specs=[VMEM] * len(shifts),
            compiler_params=params,
            name="pack",
        )(near(image))

    blocks = {("m", order[0]): first}
    blocks.update(zip([("m", k) for k in order[1:] + [0]], pack(moving, order[1:] + [0])))
    blocks.update(zip([("f", k) for k in later + [0]], pack(fixed, later + [0])))
    turns = [("m", k) for k in order] + [("f", k) for k in later]
    got = {
        (image, k): lax.ppermute(
            blocks[image, k], "tile", [(i, (i + k) % n) for i in range(n)]
        )
        for image, k in turns
    }
    moved = [got["m", k] for k in order] + [blocks["m", 0]]
    fixes = [got["f", k] for k in later] + [blocks["f", 0]]
    parts = pl.pallas_call(
        functools.partial(moving_kernel, n, rows, width),
        out_shape=[plane] * 5 + [held((3, rows, strip[1]))],
        in_specs=[VMEM] * (n + 1) + [ANY] * 2,
        out_specs=[VMEM] * 6,
        scratch_shapes=[
            pltpu.VMEM((deep, width + LANES), F32),
            pltpu.VMEM((3, rows, width + 2 * LANES), BF16),
            pltpu.VMEM((3, rows, width + 2 * LANES), BF16),
            pltpu.VMEM((n, 2 * REACH + 2, deep, LANES), F32),
            pltpu.VMEM((n, deep, LANES), F32),
            pltpu.VMEM((2, n, deep, LANES), F32),
            pltpu.VMEM((5, deep, LANES), F32),
            pltpu.VMEM(offsets.shape, jnp.int32),
            pltpu.VMEM(fractions.shape, F32),
            pltpu.SemaphoreType.DMA((2,)),
        ],
        compiler_params=params,
        cost_estimate=pl.CostEstimate(
            flops=200 * rows * width, bytes_accessed=16 * rows * width, transcendentals=0
        ),
        name="moving_part",
    )(*map(near, (*moved, fixes[-1])), far(offsets), far(fractions))
    per = rows // STEPS
    return pl.pallas_call(
        functools.partial(final_kernel, n, rows, width),
        out_shape=jax.ShapeDtypeStruct((rows, width), F32),
        in_specs=[VMEM] * (2 * n + 4),
        out_specs=ANY,
        scratch_shapes=[
            pltpu.VMEM((per, width + LANES), F32),
            pltpu.VMEM((per, width + LANES), F32),
            pltpu.VMEM((3, per, width), BF16),
            pltpu.VMEM((3, per, width), BF16),
            pltpu.VMEM((2, per, width), F32),
            pltpu.VMEM((n - 1, 5, per + 2 * HALO, LANES), F32),
            pltpu.VMEM((rows, width), F32),
            pltpu.SemaphoreType.DMA((STEPS,)),
        ],
        compiler_params=params,
        name="final_part",
    )(*map(near, (*fixes[:-1], *(moved[order.index(k)] for k in later), *parts)))


def solution(mesh):
    placed = (
        P("pair", "tile"),
        P("pair", "tile"),
        P(None, ("pair", "tile"), None),
        P(None, ("pair", "tile"), None),
    )
    return jax.shard_map(
        functools.partial(on_device, mesh.shape["tile"]),
        mesh=mesh,
        in_specs=placed,
        out_specs=P(("pair", "tile"), None),
        check_vma=False,
    )
```

```python
import functools

import jax
import jax.numpy as jnp
from jax import lax
from jax.experimental import pallas as pl
from jax.experimental.pallas import tpu as pltpu
from jax.sharding import PartitionSpec as P

RADIUS = 4
REACH = 3
HALO = max(RADIUS, REACH + 1)
LANES = 128
SUB = 8
F32 = jnp.float32
BF16 = jnp.bfloat16
ROOM = 28 * 2**20


PIECES = 3
STEPS = 1
MOVING_ORDER = (2, 1, 3)
FIXED_ORDER = (2, 1, 3)


def hops(n, first=(2, 1, 3)):
    return list(first) if n == 4 else list(range(1, n))


def pack_band(strip, base, out, band, n, rows):
    start = pl.multiple_of(band * rows - base, SUB)
    size = strip.shape[0]
    top = strip[pl.ds(pl.multiple_of(jnp.maximum(start - SUB, 0), SUB), SUB), :]
    out[0:HALO, :] = jnp.where(band > 0, top, 0.0)[SUB - HALO :, :]
    out[HALO : HALO + rows, :] = strip[pl.ds(start, rows), :]
    low = strip[pl.ds(pl.multiple_of(jnp.minimum(start + rows, size - SUB), SUB), SUB), :]
    out[HALO + rows :, :] = jnp.where(band < n - 1, low, 0.0)[:HALO, :]


def first_kernel(n, rows, pieces, moving, out, window, sem):
    band = lax.rem(lax.axis_index("tile") + hops(n, MOVING_ORDER)[0], n)
    size = window.shape[0]
    base = pl.multiple_of(jnp.clip(band * rows - SUB, 0, n * rows - size), SUB)
    per = size // pieces
    copies = [
        pltpu.make_async_copy(
            moving.at[pl.ds(pl.multiple_of(base + i * per, SUB), per), :],
            window.at[pl.ds(i * per, per), :],
            sem.at[i],
        )
        for i in range(pieces)
    ]
    for copy in copies:
        copy.start()
    for copy in copies:
        copy.wait()
    pack_band(window, base, out, band, n, rows)


def pack_kernel(n, rows, shifts, strip, *outs):
    me = lax.axis_index("tile")
    for out, k in zip(outs, shifts):
        pack_band(strip, 0, out, lax.rem(me + k, n), n, rows)


def row_sums(ref, out, rows):
    for g in range((rows + SUB) // SUB):
        y = g * SUB
        last = min(SUB, rows + 6 - y)
        out[y : y + last, :] = (
            ref[y : y + last, :] + ref[y + 1 : y + 1 + last, :] + ref[y + 2 : y + 2 + last, :]
        )

    def total(y, size):
        return out[y : y + size, :] + out[y + 3 : y + 3 + size, :] + out[y + 6 : y + 6 + size, :]

    return total


def split(x):
    high = x.astype(BF16)
    rest = x - high.astype(F32)
    middle = rest.astype(BF16)
    low = (rest - middle.astype(F32)).astype(BF16)
    return high, middle, low


def put(terms, source, y, x):
    at = pl.ds(pl.multiple_of((source + 1) * LANES, LANES), LANES)
    for t, part in enumerate(split(x)):
        terms[t, y : y + x.shape[0], at] = part


def clear_ends(terms):
    zeros = jnp.zeros((terms.shape[1], LANES), BF16)
    for t in range(3):
        terms[t, :, :LANES] = zeros
        terms[t, :, terms.shape[2] - LANES :] = zeros


def lane_sums(arrays, width, size, weights):
    wide = size + 2 * LANES
    left = [
        jnp.concatenate([terms[t, :, start : start + wide] for t in range(3)], axis=1)
        for terms in arrays
        for start in range(0, width, size)
    ]
    out = jnp.dot(jnp.concatenate(left, axis=0), weights, preferred_element_type=F32)
    rows = arrays[0].shape[1]
    parts = [out[i * rows : (i + 1) * rows] for i in range(len(left))]
    count = width // size
    return [parts[i * count : (i + 1) * count] for i in range(len(arrays))]


def band_matrix(first, last, size):
    shape = (size + 2 * LANES, size)
    source = lax.broadcasted_iota(jnp.int32, shape, 0)
    target = lax.broadcasted_iota(jnp.int32, shape, 1)
    distance = source - target - LANES
    band = jnp.where((distance >= first) & (distance <= last), 1.0, 0.0).astype(BF16)
    return jnp.concatenate([band] * 3, axis=0)


def narrow(values, bit):
    return [jnp.where(bit, values[i + 4], values[i]) for i in range(4)] + [values[4]]


def fixed_row_sums(f, m, products, rows):
    for y in range(0, f.shape[0], SUB):
        x = f[y : y + SUB, :]
        products[0, y : y + SUB, :] = x * x
        products[1, y : y + SUB, :] = x * m[y : y + SUB, :]
    return [
        row_sums(ref, products.at[2 + which], rows)
        for which, ref in enumerate((f, products.at[0], products.at[1]))
    ]


def lane_windows(terms, out):
    _, rows, width = terms.shape
    blocks = width // LANES
    size = LANES * (2 if blocks % 2 == 0 else 1)
    source = lax.broadcasted_iota(jnp.int32, (size, size), 0)
    target = lax.broadcasted_iota(jnp.int32, (size, size), 1)
    near_by = (source - target <= RADIUS) & (target - source <= RADIUS)
    inside = jnp.where(near_by, 1.0, 0.0).astype(BF16)
    source = lax.broadcasted_iota(jnp.int32, (2 * LANES, 2 * LANES), 0)
    target = lax.broadcasted_iota(jnp.int32, (2 * LANES, 2 * LANES), 1)
    near_by = (source - target <= RADIUS) & (target - source <= RADIUS)
    other = (source < LANES) != (target < LANES)
    across = jnp.where(near_by & other, 1.0, 0.0).astype(BF16)

    def times(starts, wide, weights):
        left = [
            jnp.concatenate([terms[t, :, start : start + wide] for t in range(3)], axis=1)
            for start in starts
        ]
        got = jnp.dot(
            jnp.concatenate(left, axis=0),
            jnp.concatenate([weights] * 3, axis=0),
            preferred_element_type=F32,
        )
        return [got[i * rows : (i + 1) * rows] for i in range(len(left))]

    starts = list(range(0, width, size))
    for start, part in zip(starts, times(starts, size, inside)):
        out[:, start : start + size] = part
    starts = [start - LANES for start in starts[1:]]
    if starts:
        for start, part in zip(starts, times(starts, 2 * LANES, across)):
            at = slice(start, start + 2 * LANES)
            out[:, at] = out[:, at] + part


def moving_kernel(n, rows, width, *refs):
    blocks, fixed, offsets, fractions = refs[:n], refs[n], refs[n + 1], refs[n + 2]
    base, linear, square, msum, mvar, own = refs[n + 3 : n + 9]
    image, sums, squares, shifted, sq, three, products, obuf, fbuf, sem = refs[n + 9 :]
    me = lax.axis_index("tile")
    copies = [
        pltpu.make_async_copy(offsets, obuf, sem.at[0]),
        pltpu.make_async_copy(fractions, fbuf, sem.at[1]),
    ]
    for copy in copies:
        copy.start()
    for which, total in enumerate(fixed_row_sums(fixed, blocks[n - 1], products, rows)):
        own[which] = total(0, rows)
    deep = rows + 2 * HALO
    inv = 1.0 / float((2 * RADIUS + 1) ** 2)
    for terms in (sums, squares):
        clear_ends(terms)
    for place, k in enumerate(hops(n, MOVING_ORDER) + [0]):
        block = blocks[place]
        source = lax.rem(me - k + n, n)
        for y in range(0, deep, 2 * SUB):
            size = min(2 * SUB, deep - y)
            x = block[y : y + size, :]
            sq[place, y : y + size, :] = x * x
            at = pl.ds(pl.multiple_of(source * LANES, LANES), LANES)
            image[y : y + size, at] = x
        for which, (ref, terms) in enumerate(((block, sums), (sq.at[place], squares))):
            total = row_sums(ref, three.at[which, place], rows)
            for y in range(0, rows, 2 * SUB):
                put(terms, source, y, total(y, 2 * SUB))
    size = LANES * (2 if n % 2 == 0 else 1)
    window = band_matrix(-RADIUS, RADIUS, size)
    totals, seconds = lane_sums((sums, squares), width, size, window)
    for place, (total, second) in enumerate(zip(totals, seconds)):
        at = pl.ds(place * size, size)
        msum[:, at] = total
        mvar[:, at] = second - total * total * inv
    image[:, width:] = jnp.zeros((deep, LANES), F32)
    for y in range(0, deep, SUB):
        x = image[y : y + SUB, :]
        for c in range(-REACH, REACH + 2):
            turned = pltpu.roll(x, (-c) % x.shape[1], 1) if c else x
            for block in range(n):
                shifted[block, c + REACH, y : y + SUB, :] = turned[
                    :, block * LANES : (block + 1) * LANES
                ]
    span = 2 * REACH + 2

    def unit(s, y0):
        at = pl.ds(s * LANES, LANES)
        down = obuf[0, y0 : y0 + SUB, at] + REACH
        along = obuf[1, y0 : y0 + SUB, at] + REACH
        down_bits = [down >= 4, (down & 2) == 2, (down & 1) == 1]
        along_bits = [along >= 4, (along & 2) == 2, (along & 1) == 1]

        def load(r):
            e = y0 + r + HALO - REACH
            return [shifted[s, c, e : e + SUB, :] for c in range(span)]

        grid = []
        for r in range(5):
            line = load(r)
            if r < 4:
                line = [jnp.where(down_bits[0], b, a) for a, b in zip(line, load(r + 4))]
            grid.append(narrow(line, along_bits[0]))
        for place, step in ((1, 2), (2, 1)):
            across_bit, down_bit = along_bits[place], down_bits[place]
            lines = [
                [jnp.where(down_bit, b, a) for a, b in zip(grid[r], grid[r + step])]
                for r in range(step + 1)
            ]
            grid = [
                [jnp.where(across_bit, line[i + step], line[i]) for i in range(step + 1)]
                for line in lines
            ]
        (top_left, top_right), (bottom_left, bottom_right) = grid
        rf = fbuf[0, y0 : y0 + SUB, at]
        cf = fbuf[1, y0 : y0 + SUB, at]
        across = top_right - top_left
        base[y0 : y0 + SUB, at] = top_left
        linear[y0 : y0 + SUB, at] = cf * across + rf * (bottom_left - top_left)
        square[y0 : y0 + SUB, at] = (rf * cf) * ((bottom_right - bottom_left) - across)

    for copy in copies:
        copy.wait()
    for s in range(n):
        for g in range(rows // SUB):
            unit(s, g * SUB)


def final_kernel(n, rows, width, *refs):
    per = rows // STEPS
    sem = refs[-1]

    def result(step):
        at = pl.ds(pl.multiple_of(step * per, SUB), per)
        obuf, out = refs[-2], refs[2 * n + 4]
        return pltpu.make_async_copy(obuf.at[at, :], out.at[at, :], sem.at[step])

    def one(step, carry):
        final_rows(n, per, width, pl.multiple_of(step * per, SUB), refs)
        result(step).start()
        return carry

    lax.fori_loop(0, STEPS, one, 0)
    for step in range(STEPS):
        result(step).wait()


def final_rows(n, rows, width, start, refs):
    deep = pl.ds(start, rows + 2 * HALO)
    here = pl.ds(start, rows)
    fixed = [ref.at[deep, :] for ref in refs[: n - 1]]
    moving = [ref.at[deep, :] for ref in refs[n - 1 : 2 * n - 2]]
    base, linear, square, msum, mvar = [ref.at[here, :] for ref in refs[2 * n - 2 : 2 * n + 3]]
    own = refs[2 * n + 3].at[:, here, :]
    summed, triple, square_terms, cross_terms, windows, products, obuf = refs[2 * n + 5 : -1]
    obuf = obuf.at[here, :]
    me = lax.axis_index("tile")
    inv = 1.0 / float((2 * RADIUS + 1) ** 2)
    extent = width + LANES
    summed[:, width:] = jnp.zeros((rows, LANES), F32)
    blocks = [(me, [lambda y, size, w=w: own[w, y : y + size, :] for w in range(3)])]
    for place, k in enumerate(hops(n, FIXED_ORDER)):
        totals = fixed_row_sums(fixed[place], moving[place], products.at[place], rows)
        blocks.append((lax.rem(me - k + n, n), totals))

    def places():
        for source, totals in blocks:
            yield pl.ds(pl.multiple_of(source * LANES, LANES), LANES), totals

    for at, totals in places():
        for y in range(0, rows, SUB):
            summed[y : y + SUB, at] = totals[0](y, SUB)
    for y in range(0, rows, SUB):
        x = summed[y : y + SUB, :]
        triple[y : y + SUB, :] = x + pltpu.roll(x, 1, 1) + pltpu.roll(x, extent - 1, 1)
    for which, terms in enumerate((square_terms, cross_terms)):
        for at, totals in places():
            for y in range(0, rows, 2 * SUB):
                for t, part in enumerate(split(totals[1 + which](y, 2 * SUB))):
                    terms[t, y : y + 2 * SUB, at] = part
        lane_windows(terms, windows.at[which])
    for y in range(0, rows, SUB):
        at = slice(y, y + SUB)
        x = triple[at, :]
        fsum = (x + pltpu.roll(x, 3, 1) + pltpu.roll(x, extent - 3, 1))[:, :width]
        fvar = windows[0, at, :] - fsum * fsum * inv
        cov = windows[1, at, :] - fsum * msum[at, :] * inv
        conf = 0.5 + 0.5 * (cov * lax.rsqrt(fvar * mvar[at, :] + 0.001))
        obuf[at, :] = base[at, :] + conf * (linear[at, :] + conf * square[at, :])


VMEM = pl.BlockSpec(memory_space=pltpu.VMEM)
ANY = pl.BlockSpec(memory_space=pl.ANY)


def held(shape):
    return pltpu.VMEM(shape, F32)


def near(x):
    return pltpu.with_memory_space_constraint(x, pltpu.VMEM)


def far(x):
    return pltpu.with_memory_space_constraint(x, pltpu.HBM)


def on_device(n, fixed, moving, offsets, fractions):
    rows, width = offsets.shape[1:]
    strip = moving.shape
    deep = rows + 2 * HALO
    band = held((deep, strip[1]))
    plane = held((rows, width))
    params = pltpu.CompilerParams(vmem_limit_bytes=ROOM)
    pieces = PIECES
    first = pl.pallas_call(
        functools.partial(first_kernel, n, rows, pieces),
        out_shape=band,
        in_specs=[ANY],
        out_specs=VMEM,
        scratch_shapes=[
            pltpu.VMEM((rows + 2 * SUB, strip[1]), F32),
            pltpu.SemaphoreType.DMA((pieces,)),
        ],
        compiler_params=params,
        name="first",
    )(far(moving))
    order, later = hops(n, MOVING_ORDER), hops(n, FIXED_ORDER)

    def pack(image, shifts):
        return pl.pallas_call(
            functools.partial(pack_kernel, n, rows, shifts),
            out_shape=[band] * len(shifts),
            in_specs=[VMEM],
            out_specs=[VMEM] * len(shifts),
            compiler_params=params,
            name="pack",
        )(near(image))

    blocks = {("m", order[0]): first}
    blocks.update(zip([("m", k) for k in order[1:] + [0]], pack(moving, order[1:] + [0])))
    blocks.update(zip([("f", k) for k in later + [0]], pack(fixed, later + [0])))
    turns = [("m", k) for k in order] + [("f", k) for k in later]
    got = {
        (image, k): lax.ppermute(
            blocks[image, k], "tile", [(i, (i + k) % n) for i in range(n)]
        )
        for image, k in turns
    }
    moved = [got["m", k] for k in order] + [blocks["m", 0]]
    fixes = [got["f", k] for k in later] + [blocks["f", 0]]
    parts = pl.pallas_call(
        functools.partial(moving_kernel, n, rows, width),
        out_shape=[plane] * 5 + [held((3, rows, strip[1]))],
        in_specs=[VMEM] * (n + 1) + [ANY] * 2,
        out_specs=[VMEM] * 6,
        scratch_shapes=[
            pltpu.VMEM((deep, width + LANES), F32),
            pltpu.VMEM((3, rows, width + 2 * LANES), BF16),
            pltpu.VMEM((3, rows, width + 2 * LANES), BF16),
            pltpu.VMEM((n, 2 * REACH + 2, deep, LANES), F32),
            pltpu.VMEM((n, deep, LANES), F32),
            pltpu.VMEM((2, n, deep, LANES), F32),
            pltpu.VMEM((5, deep, LANES), F32),
            pltpu.VMEM(offsets.shape, jnp.int32),
            pltpu.VMEM(fractions.shape, F32),
            pltpu.SemaphoreType.DMA((2,)),
        ],
        compiler_params=params,
        cost_estimate=pl.CostEstimate(
            flops=200 * rows * width, bytes_accessed=16 * rows * width, transcendentals=0
        ),
        name="moving_part",
    )(*map(near, (*moved, fixes[-1])), far(offsets), far(fractions))
    per = rows // STEPS
    return pl.pallas_call(
        functools.partial(final_kernel, n, rows, width),
        out_shape=jax.ShapeDtypeStruct((rows, width), F32),
        in_specs=[VMEM] * (2 * n + 4),
        out_specs=ANY,
        scratch_shapes=[
            pltpu.VMEM((per, width + LANES), F32),
            pltpu.VMEM((per, width + LANES), F32),
            pltpu.VMEM((3, per, width), BF16),
            pltpu.VMEM((3, per, width), BF16),
            pltpu.VMEM((2, per, width), F32),
            pltpu.VMEM((n - 1, 5, per + 2 * HALO, LANES), F32),
            pltpu.VMEM((rows, width), F32),
            pltpu.SemaphoreType.DMA((STEPS,)),
        ],
        compiler_params=params,
        name="final_part",
    )(*map(near, (*fixes[:-1], *(moved[order.index(k)] for k in later), *parts)))


def solution(mesh):
    placed = (
        P("pair", "tile"),
        P("pair", "tile"),
        P(None, ("pair", "tile"), None),
        P(None, ("pair", "tile"), None),
    )
    return jax.shard_map(
        functools.partial(on_device, mesh.shape["tile"]),
        mesh=mesh,
        in_specs=placed,
        out_specs=P(("pair", "tile"), None),
        check_vma=False,
    )
```
